512 devices in a mesh: section: 64 (over x, y, z_hi), seq: 8 (over z_lo, core).
Axes of the slice: x: 4, y: 4, z: 16 (z_hi: 4, z_lo: 4; z = z_hi * 4 + z_lo), core: 2. Of those that a mesh axis runs over, the one named last changes fastest.
Arguments:
- section_input: bfloat16 [64, 1024, 4096], P('section', 'seq'), may hold values from -6 to 6
- norm_gain: float32 [64, 4096], P('section'), may hold values from 0.5 to 1.5
- w_query: bfloat16 [64, 4096, 1024], P('section', 'seq'), may hold values from -1 to 1
- w_keyval: bfloat16 [64, 4096, 256], P('section', 'seq'), may hold values from -1 to 1
- w_out: bfloat16 [64, 1024, 4096], P('section', None, 'seq'), may hold values from -0.1875 to 0.1875
- down_grads: bfloat16 [64, 4096, 128], P('section', 'seq'), may hold values from -6 to 6
- up_grads: bfloat16 [64, 4096, 128], P('section', 'seq'), may hold values from -6 to 6
Outputs:
- section_output: bfloat16 [64, 1024, 4096], P('section', 'seq')
- grad_sum: bfloat16 [64, 4096, 128], P('section', 'seq')
The draws below stay inside these ranges and needn't reach their ends.
All inputs are finite; a program needn't handle non-finite values.
Results may differ from the reference program's by a relative error of at most 0.015.
Values may be sent and summed in bfloat16 or wider, within the bound.
No kernel may reach another device: no remote copies, remote signals or barrier semaphores. Data moves between devices by JAX's collectives and lax.ppermute only.
A program may use at most 64 MiB of HBM per device.

```python
import math
import jax
import jax.numpy as jnp
from jax import lax

D = 4096
HD = 128
QH = 8
QW = 1024
SEQ_LEN = 1024
SECTIONS = 64
N_SEQ = 8


def draw_section_input(key, part):
    noise_key = jax.random.fold_in(key, 11)
    shape_all = (SECTIONS, SEQ_LEN, D)
    values_all = jnp.clip(jax.random.normal(noise_key, shape_all, jnp.float32), -6.0, 6.0)
    return values_all.astype(jnp.bfloat16)


def draw_w_query(key, part):
    noise_key = jax.random.fold_in(key, 13)
    shape_all = (SECTIONS, D, QW)
    values_all = jnp.clip(jax.random.normal(noise_key, shape_all, jnp.float32), -6.0, 6.0) / math.sqrt(D)
    return values_all.astype(jnp.bfloat16)


def draw_w_keyval(key, part):
    noise_key = jax.random.fold_in(key, 17)
    shape_all = (SECTIONS, D, 2 * HD)
    values_all = jnp.clip(jax.random.normal(noise_key, shape_all, jnp.float32), -6.0, 6.0) / math.sqrt(D)
    return values_all.astype(jnp.bfloat16)


def block_scale(key, extent, cuts, least, largest):
    def one(dim, blocks):
        draws = jax.random.uniform(jax.random.fold_in(jax.random.fold_in(key, 6), dim), (blocks,), jnp.float32, least / len(cuts), largest / len(cuts))
        return jnp.repeat(jnp.exp(draws), extent[dim] // blocks).reshape((-1,) + (1,) * (len(extent) - dim - 1))

    loudness = one(*cuts[0])
    for cut in cuts[1:]:
        loudness = loudness * one(*cut)
    return loudness


def centred(key, extent, deviation, limit, cuts=(), kind=jnp.bfloat16):
    result = deviation * jax.random.normal(key, extent, jnp.float32)
    if cuts:
        result = result * block_scale(key, extent, cuts, -0.22, 0.18)
    return jnp.clip(result, -limit, limit).astype(kind)


def setup_inputs(seed: int = 0) -> dict:
    seeds = jax.random.split(jax.random.key(seed), 8)
    section_input = draw_section_input(jax.random.fold_in(seeds[7], 71), 0)
    norm_gain = jnp.clip(1.0 + 0.1 * jax.random.normal(seeds[1], (SECTIONS, D), jnp.float32), 0.5, 1.5)
    w_query = draw_w_query(jax.random.fold_in(seeds[7], 71), 0)
    w_keyval = draw_w_keyval(jax.random.fold_in(seeds[7], 71), 0)
    w_out = centred(seeds[4], (SECTIONS, QW, D), QW ** -0.5, 0.1875, ((0, 64), (2, 8)))
    down_grads = centred(seeds[5], (SECTIONS, D, HD), 1.0, 6.0, ((0, 64), (1, 8)))
    up_grads = centred(seeds[6], (SECTIONS, D, HD), 1.0, 6.0, ((0, 64), (1, 8)))
    return {"section_input": section_input, "norm_gain": norm_gain, "w_query": w_query, "w_keyval": w_keyval, "w_out": w_out, "down_grads": down_grads, "up_grads": up_grads}


def rotate(values, positions):
    halfway = values.shape[1] // 2
    frequency = 10000.0 ** (-(jnp.arange(halfway, dtype=jnp.float32) * 2.0 / values.shape[1]))
    angles = positions[:, None] * frequency[None, :]
    cosine = jnp.cos(angles)
    sine_part = jnp.sin(angles)
    leading = values[:, :halfway]
    trailing = values[:, halfway:]
    return jnp.concatenate([leading * cosine - trailing * sine_part, trailing * cosine + leading * sine_part], axis=1)

def attend_head(queries, key_rows, value_rows):
    length = queries.shape[0]
    scores = jnp.dot(queries, key_rows.T, preferred_element_type=jnp.float32) * (1.0 / math.sqrt(HD))
    row_ids = jnp.arange(length, dtype=jnp.int32)[:, None]
    col_ids = jnp.arange(length, dtype=jnp.int32)[None, :]
    scores = jnp.where(col_ids <= row_ids, scores, jnp.float32(-1e+30))
    highest = lax.optimization_barrier(jnp.max(scores, axis=1, keepdims=True))
    raised = jnp.exp(scores - highest)
    probs = (raised / lax.optimization_barrier(jnp.sum(raised, axis=1, keepdims=True))).astype(jnp.bfloat16)
    return jnp.dot(probs, value_rows, preferred_element_type=jnp.float32).astype(jnp.bfloat16)

def section_layer(operands):
    section_rows, gain_row, query_weight, keyval_weight, output_weight = operands
    widened = section_rows.astype(jnp.float32)
    normed = (widened * lax.rsqrt(lax.optimization_barrier(jnp.mean(widened * widened, axis=1, keepdims=True)) + 1e-05) * gain_row[None, :]).astype(jnp.bfloat16)
    width_block = D // N_SEQ
    query_sum = jnp.zeros((SEQ_LEN, QW), jnp.float32)
    for member in range(N_SEQ):
        partial_term = jnp.dot(normed[:, member * width_block:(member + 1) * width_block], query_weight[member * width_block:(member + 1) * width_block], preferred_element_type=jnp.float32)
        rounded = lax.optimization_barrier(partial_term.astype(jnp.bfloat16))
        query_sum = query_sum + rounded.astype(jnp.float32)
    keyval = jnp.dot(normed, keyval_weight, preferred_element_type=jnp.float32)
    positions = jnp.arange(SEQ_LEN, dtype=jnp.float32)
    key_rows = rotate(keyval[:, :HD], positions).astype(jnp.bfloat16)
    value_rows = keyval[:, HD:].astype(jnp.bfloat16)
    outputs = []
    for head in range(QH):
        queries = rotate(query_sum[:, head * HD:(head + 1) * HD], positions).astype(jnp.bfloat16)
        outputs.append(attend_head(queries, key_rows, value_rows))
    joined = jnp.concatenate(outputs, axis=1)
    attn = jnp.dot(joined, output_weight, preferred_element_type=jnp.float32).astype(jnp.bfloat16)
    return (widened + attn.astype(jnp.float32)).astype(jnp.bfloat16)

def reference(section_input, norm_gain, w_query, w_keyval, w_out, down_grads, up_grads):
    layer_out = lax.map(section_layer, (section_input, norm_gain, w_query, w_keyval, w_out))
    section_output = layer_out.reshape(SECTIONS // 2, 2, SEQ_LEN, D)[:, ::-1].reshape(SECTIONS, SEQ_LEN, D)
    grad_sum = (down_grads.astype(jnp.float32) + up_grads[::-1].astype(jnp.float32)).astype(jnp.bfloat16)
    return (section_output, grad_sum)
```

```python
import math

import jax
import jax.numpy as jnp
from jax import lax
from jax.experimental import pallas as pl
from jax.experimental.pallas import tpu as pltpu
from jax.sharding import PartitionSpec as P

VMEM_LIMIT = 40 * 1024 * 1024


def exchange(x, flip):
    size = lax.axis_size("seq")
    return lax.ppermute(x, "seq", [(i, i ^ flip) for i in range(size)])


def across(x, flip):
    sections, size = lax.axis_size("section"), lax.axis_size("seq")
    pairs = [
        (s * size + i, (s ^ 1) * size + (i ^ flip)) for s in range(sections) for i in range(size)
    ]
    return lax.ppermute(x, ("section", "seq"), pairs)


def piece(place, k):
    return (place % 4) ^ (2 * (k // 2) + k % 2)


def call(kernel, outs, *args):
    return pl.pallas_call(
        kernel,
        out_shape=outs,
        in_specs=[pl.BlockSpec(memory_space=pltpu.SMEM)]
        + [pl.BlockSpec(memory_space=pltpu.VMEM)] * (len(args) - 1),
        compiler_params=pltpu.CompilerParams(vmem_limit_bytes=VMEM_LIMIT),
    )(*args)


def project_kernel(place_ref, own_ref, far_ref, gain_ref, w0, w1, w2, w3, near_out, far_out):
    place = place_ref[0]
    half = place // 4
    near = None
    far = None
    width = w0.shape[0]
    for k, weight in enumerate((w0, w1, w2, w3)):
        part = piece(place, k)
        start = pl.multiple_of(part * width, width)
        whole = pl.multiple_of((half * 4 + part) * width, width)
        gain = gain_ref[:, pl.ds(whole, width)]
        a = (own_ref[:, pl.ds(whole, width)].astype(jnp.float32) * gain).astype(jnp.bfloat16)
        b = (far_ref[:, pl.ds(start, width)].astype(jnp.float32) * gain).astype(jnp.bfloat16)
        w = weight[...]
        a = jnp.dot(a, w, preferred_element_type=jnp.float32)
        b = jnp.dot(b, w, preferred_element_type=jnp.float32)
        near = a if near is None else near + a
        far = b if far is None else far + b
    near_out[...] = near
    far_out[...] = far.astype(jnp.bfloat16)


def rope(values, cosine, sine):
    return values * cosine + pltpu.roll(values, values.shape[1] // 2, axis=1) * sine


def keyval_kernel(near_ref, far_ref, scale_ref, cos_ref, sin_ref, out_ref):
    total = (near_ref[...] + far_ref[...].astype(jnp.float32)) * scale_ref[...]
    size = total.shape[1] // 2
    out_ref[:, :size] = rope(total[:, :size], cos_ref[...], sin_ref[...]).astype(jnp.bfloat16)
    out_ref[:, size:] = total[:, size:].astype(jnp.bfloat16)


def attend_kernel(place_ref, near_ref, far_ref, scale_ref, cos_ref, sin_ref, kv_ref, out_ref):
    rows, width = near_ref.shape
    length = kv_ref.shape[0]
    size = kv_ref.shape[1] // 2
    keys = kv_ref[:, :size]
    values = kv_ref[:, size:]
    row_ids = place_ref[0] * rows + lax.broadcasted_iota(jnp.int32, (rows, length), 0)
    keep = lax.broadcasted_iota(jnp.int32, (rows, length), 1) <= row_ids
    scale = scale_ref[...]
    cosine = cos_ref[...]
    sine = sin_ref[...]
    for head in range(width // size):
        cols = slice(head * size, (head + 1) * size)
        total = (near_ref[:, cols] + far_ref[:, cols].astype(jnp.float32)) * scale
        query = rope(total, cosine, sine).astype(jnp.bfloat16)
        scores = lax.dot_general(
            query, keys, (((1,), (1,)), ((), ())), preferred_element_type=jnp.float32
        ) * (1.0 / math.sqrt(size))
        scores = jnp.where(keep, scores, jnp.float32(-1e30))
        raised = jnp.exp(scores - jnp.max(scores, axis=1, keepdims=True))
        total = jnp.sum(raised, axis=1, keepdims=True)
        mixed = jnp.dot(raised.astype(jnp.bfloat16), values, preferred_element_type=jnp.float32)
        out_ref[:, cols] = (mixed / total).astype(jnp.bfloat16)


def output_kernel(
    place_ref, heads_ref, far_heads_ref, own_ref, far_ref, w0, w1, w2, w3, near_out, far_out
):
    place = place_ref[0]
    half = place // 4
    width = w0.shape[1]
    near = heads_ref[...]
    far = far_heads_ref[...]
    for k, weight in enumerate((w0, w1, w2, w3)):
        part = piece(place, k)
        start = pl.multiple_of(part * width, width)
        whole = pl.multiple_of((half * 4 + part) * width, width)
        w = weight[...]
        a = jnp.dot(near, w, preferred_element_type=jnp.float32)
        b = jnp.dot(far, w, preferred_element_type=jnp.float32)
        a = a + own_ref[:, pl.ds(whole, width)].astype(jnp.float32)
        b = b + far_ref[:, pl.ds(start, width)].astype(jnp.float32)
        near_out[:, pl.ds(start, width)] = a.astype(jnp.bfloat16)
        far_out[:, pl.ds(start, width)] = b.astype(jnp.bfloat16)


def gathered(own):
    second = exchange(own, 2)
    return own, exchange(own, 1), second, exchange(second, 1)


def shards(section_input, norm_gain, w_query, w_keyval, w_out, down_grads, up_grads):
    rows = section_input[0]
    tokens, features = rows.shape
    seq = lax.axis_index("seq")
    half = seq // 4
    place = seq.astype(jnp.int32)[None]
    far_rows = exchange(
        lax.dynamic_slice_in_dim(rows, (1 - half) * (features // 2), features // 2, axis=1), 4
    )
    keyval_weights = gathered(w_keyval[0])
    query_weights = gathered(w_query[0])
    output_weights = gathered(w_out[0])
    widened = rows.astype(jnp.float32)
    scale = lax.rsqrt(jnp.mean(widened * widened, axis=1, keepdims=True) + 1e-05)
    size = w_keyval.shape[2] // 2
    frequency = 10000.0 ** (-(jnp.arange(size // 2, dtype=jnp.float32) * 2.0 / size))
    positions = (seq * tokens + jnp.arange(tokens)).astype(jnp.float32)
    angles = positions[:, None] * frequency[None, :]
    cosine = jnp.cos(angles)
    sine = jnp.sin(angles)
    cosine = jnp.concatenate([cosine, cosine], axis=1)
    sine = jnp.concatenate([-sine, sine], axis=1)

    def partials(weights):
        width = weights[0].shape[1]
        outs = (
            jax.ShapeDtypeStruct((tokens, width), jnp.float32),
            jax.ShapeDtypeStruct((tokens, width), jnp.bfloat16),
        )
        return call(project_kernel, outs, place, rows, far_rows, norm_gain, *weights)

    near, far = partials(keyval_weights)
    keyval = pl.pallas_call(
        keyval_kernel, out_shape=jax.ShapeDtypeStruct((tokens, 2 * size), jnp.bfloat16)
    )(near, exchange(far, 4), scale, cosine, sine)
    keyval = lax.all_gather(keyval, "seq", axis=0, tiled=True)
    near, far = partials(query_weights)
    heads = call(
        attend_kernel,
        jax.ShapeDtypeStruct(near.shape, jnp.bfloat16),
        place, near, exchange(far, 4), scale, cosine, sine, keyval,
    )
    out = jax.ShapeDtypeStruct((tokens, features // 2), jnp.bfloat16)
    near, far = call(
        output_kernel, (out, out), place, heads, exchange(heads, 4), rows, far_rows, *output_weights
    )
    near = across(near, 0)
    far = across(far, 4)
    first = half == 0
    received = jnp.concatenate(
        [jnp.where(first, near, far), jnp.where(first, far, near)], axis=1
    )
    sections = lax.axis_size("section")
    mirrored = lax.ppermute(up_grads[0], "section", [(i, sections - 1 - i) for i in range(sections)])
    grad_total = (down_grads[0].astype(jnp.float32) + mirrored.astype(jnp.float32)).astype(
        jnp.bfloat16
    )
    return (received[None], grad_total[None])


def solution(mesh):
    return jax.shard_map(
        shards,
        mesh=mesh,
        in_specs=(
            P("section", "seq", None),
            P("section", None),
            P("section", "seq", None),
            P("section", "seq", None),
            P("section", None, "seq"),
            P("section", "seq", None),
            P("section", "seq", None),
        ),
        out_specs=(P("section", "seq", None), P("section", "seq", None)),
        check_vma=False,
    )
```

```python
import math

import jax
import jax.numpy as jnp
from jax import lax
from jax.experimental import pallas as pl
from jax.experimental.pallas import tpu as pltpu
from jax.sharding import PartitionSpec as P

LEADING = 64
VMEM_LIMIT = 8 * 1024 * 1024


def exchange(x, flip):
    size = lax.axis_size("seq")
    return lax.ppermute(x, "seq", [(i, i ^ flip) for i in range(size)])


def across(x, flip):
    sections, size = lax.axis_size("section"), lax.axis_size("seq")
    pairs = [
        (s * size + i, (s ^ 1) * size + (i ^ flip)) for s in range(sections) for i in range(size)
    ]
    return lax.ppermute(x, ("section", "seq"), pairs)


def piece(place, k):
    return (place % 4) ^ (2 * (k // 2) + k % 2)


def after(x, *others):
    return lax.optimization_barrier((x,) + others)[0]


def call(kernel, outs, *args):
    return pl.pallas_call(
        kernel,
        out_shape=outs,
        in_specs=[pl.BlockSpec(memory_space=pltpu.SMEM)]
        + [pl.BlockSpec(memory_space=pltpu.VMEM)] * (len(args) - 1),
        compiler_params=pltpu.CompilerParams(vmem_limit_bytes=VMEM_LIMIT),
        cost_estimate=pl.CostEstimate(flops=1, transcendentals=0, bytes_accessed=1),
    )(*args)


def scale_kernel(place_ref, rows_ref, out_ref):
    rows = rows_ref[...].astype(jnp.float32)
    scale = lax.rsqrt(jnp.mean(rows * rows, axis=1, keepdims=True) + 1e-05)
    out_ref[...] = jnp.broadcast_to(scale, out_ref.shape)


def dot(a, b):
    return jnp.dot(a, b, preferred_element_type=jnp.float32)


def project(place, own_ref, far_ref, gain_ref, weights, pieces):
    half = place // 4
    near = None
    far = None
    for k, weight in zip(pieces, weights):
        width = weight.shape[0]
        part = piece(place, k)
        start = pl.multiple_of(part * width, width)
        whole = pl.multiple_of((half * 4 + part) * width, width)
        gain = gain_ref[:, pl.ds(whole, width)]
        a = (own_ref[:, pl.ds(whole, width)].astype(jnp.float32) * gain).astype(jnp.bfloat16)
        b = (far_ref[:, pl.ds(start, width)].astype(jnp.float32) * gain).astype(jnp.bfloat16)
        w = weight[...]
        total = dot(jnp.concatenate([a, b], axis=0), w)
        a, b = total[: a.shape[0]], total[a.shape[0] :]
        near = a if near is None else near + a
        far = b if far is None else far + b
    return near, far


def project_kernel(place_ref, own_ref, far_ref, gain_ref, w0, w1, w2, w3, near_out, far_out):
    near, far = project(
        place_ref[0], own_ref, far_ref, gain_ref, (w0, w1, w2, w3), (0, 1, 2, 3)
    )
    near_out[...] = near
    far_out[...] = far.astype(jnp.bfloat16)


def rope(values, cosine, sine):
    return values * cosine + pltpu.roll(values, values.shape[1] // 2, axis=1) * sine


def collect_kernel(place_ref, near_ref, far_ref, scale_ref, cos_ref, sin_ref, out_ref):
    total = near_ref[...] + far_ref[...].astype(jnp.float32)
    scale = scale_ref[...]
    size = total.shape[1] // 2
    keys = rope(total[:, :size] * scale, cos_ref[...], sin_ref[...]).astype(jnp.bfloat16)
    values = (total[:, size:] * scale).astype(jnp.bfloat16)
    for k in range(out_ref.shape[0]):
        out_ref[k, :, :size] = keys
        out_ref[k, :, size:] = values


def attend_kernel(
    place_ref, near_ref, far_ref, scale_ref, cos_ref, sin_ref, kv_ref, out_ref
):
    rows, width = near_ref.shape
    length = kv_ref.shape[0]
    size = kv_ref.shape[1] // 2
    keys = kv_ref[:, :size]
    values = kv_ref[:, size:]
    row_ids = place_ref[0] * rows
    row_ids = row_ids + lax.broadcasted_iota(jnp.int32, (rows, length), 0)
    keep = lax.broadcasted_iota(jnp.int32, (rows, length), 1) <= row_ids
    scale = scale_ref[...]
    cosine = cos_ref[...]
    sine = sin_ref[...]
    for head in range(width // size):
        cols = slice(head * size, (head + 1) * size)
        total = (near_ref[:, cols] + far_ref[:, cols].astype(jnp.float32)) * scale
        query = rope(total, cosine, sine).astype(jnp.bfloat16)
        scores = lax.dot_general(
            query, keys, (((1,), (1,)), ((), ())), preferred_element_type=jnp.float32
        ) * (1.0 / math.sqrt(size))
        scores = jnp.where(keep, scores, jnp.float32(-1e30))
        raised = jnp.exp(scores - jnp.max(scores, axis=1, keepdims=True))
        total = jnp.sum(raised, axis=1, keepdims=True)
        out_ref[:, cols] = (dot(raised.astype(jnp.bfloat16), values) / total).astype(jnp.bfloat16)


def output_kernel(far, place_ref, heads, rows_ref, *refs):
    weights, outs = refs[:4], refs[4:]
    place = place_ref[0]
    base = 0 if far else place // 4 * 4
    for k, weight in enumerate(weights):
        width = weight.shape[1]
        part = piece(place, k)
        start = pl.multiple_of(part * width, width)
        whole = pl.multiple_of((base + part) * width, width)
        total = dot(heads[...], weight[...])
        total = total + rows_ref[:, pl.ds(whole, width)].astype(jnp.float32)
        row = 0
        for out in outs:
            some = total[row : row + out.shape[0]]
            out[:, pl.ds(start, width)] = some.astype(jnp.bfloat16)
            row += out.shape[0]


def assemble_kernel(place_ref, first, second, far, out_ref):
    half = place_ref[0] // 4
    rows, width = first.shape
    near_cols = pl.ds(pl.multiple_of(half * width, width), width)
    out_ref[:rows, near_cols] = first[...]
    out_ref[rows:, near_cols] = second[...]
    out_ref[:, pl.ds(pl.multiple_of((1 - half) * width, width), width)] = far[...]


def at_row(kernel, *fixed):
    def run(*refs):
        kernel(*fixed, *refs)

    return run


def shards(section_input, norm_gain, w_query, w_keyval, w_out, down_grads, up_grads):
    rows = section_input[0]
    tokens, features = rows.shape
    size = w_keyval.shape[2] // 2
    wide = w_query.shape[2]
    bf16, f32 = jnp.bfloat16, jnp.float32
    seq = lax.axis_index("seq")
    half = seq // 4
    place = seq.astype(jnp.int32)[None]

    def array(count, columns, kind=bf16):
        return jax.ShapeDtypeStruct((count, columns), kind)

    sent = lax.dynamic_slice_in_dim(rows, (1 - half) * (features // 2), features // 2, axis=1)
    far_rows = exchange(sent, 4)
    keyval_2 = exchange(w_keyval[0], 2)
    keyval_1 = exchange(w_keyval[0], 1)
    scale = call(scale_kernel, array(tokens, size, f32), place, after(rows, sent))
    w_query = after(w_query[0], scale)
    query_2 = exchange(w_query, 2)
    query_1 = exchange(w_query, 1)
    keyval_3 = exchange(keyval_2, 1)
    query_3 = exchange(query_2, 1)
    out_1 = exchange(after(w_out[0], scale), 1)

    frequency = 10000.0 ** (-(jnp.arange(size // 2, dtype=f32) * 2.0 / size))
    positions = (seq * tokens + jnp.arange(tokens)).astype(f32)
    angles = positions[:, None] * frequency[None, :]
    cosine = jnp.cos(angles)
    sine = jnp.sin(angles)
    cosine = jnp.concatenate([cosine, cosine], axis=1)
    sine = jnp.concatenate([-sine, sine], axis=1)

    near, far = call(
        project_kernel,
        (array(tokens, 2 * size, f32), array(tokens, 2 * size)),
        place, rows, far_rows, norm_gain, w_keyval[0], keyval_1, keyval_2, keyval_3,
    )
    far = exchange(far, 4)
    query_near, query_far = call(
        project_kernel,
        (array(tokens, wide, f32), array(tokens, wide)),
        place, rows, far_rows, norm_gain, w_query, query_1, query_2, query_3,
    )
    keyval = call(
        collect_kernel,
        jax.ShapeDtypeStruct((lax.axis_size("seq"), tokens, 2 * size), bf16),
        place, near, far, scale, cosine, sine,
    )
    keyval = lax.all_to_all(keyval, "seq", split_axis=0, concat_axis=0, tiled=True)
    keyval = keyval.reshape(-1, 2 * size)
    query_far = exchange(query_far, 4)
    heads = call(
        attend_kernel,
        array(tokens, wide),
        place, query_near, query_far, scale, cosine, sine, keyval,
    )
    far_heads = exchange(heads, 4)
    out_2 = exchange(after(w_out[0], query_2), 2)
    out_3 = exchange(after(out_2, heads), 1)
    weights = w_out[0], out_1, out_2, out_3
    half_rows = array(tokens, features // 2)
    parts = tuple(array(n, features // 2) for n in (LEADING, tokens - LEADING))
    near = call(at_row(output_kernel, False), parts, place, heads, rows, *weights)
    far_heads = after(far_heads, *near)
    far = call(at_row(output_kernel, True), half_rows, place, far_heads, far_rows, *weights)
    first = across(near[0], 0)
    received = [first, across(after(near[1], first), 0), across(far, 4)]
    out = call(assemble_kernel, array(tokens, features), place, *received)
    sections = lax.axis_size("section")
    mirrored = lax.ppermute(
        after(up_grads[0], far),
        "section",
        [(i, sections - 1 - i) for i in range(sections)],
    )
    grad_total = (down_grads[0].astype(f32) + mirrored.astype(f32)).astype(bf16)
    return (out[None], grad_total[None])


def solution(mesh):
    return jax.shard_map(
        shards,
        mesh=mesh,
        in_specs=(
            P("section", "seq", None),
            P("section", None),
            P("section", "seq", None),
            P("section", "seq", None),
            P("section", None, "seq"),
            P("section", "seq", None),
            P("section", "seq", None),
        ),
        out_specs=(P("section", "seq", None), P("section", "seq", None)),
        check_vma=False,
    )
```

```python
import math

import jax
import jax.numpy as jnp
from jax import lax
from jax.experimental import pallas as pl
from jax.experimental.pallas import tpu as pltpu
from jax.sharding import PartitionSpec as P

LEADING = 64
VMEM_LIMIT = 8 * 1024 * 1024


def exchange(x, flip):
    size = lax.axis_size("seq")
    return lax.ppermute(x, "seq", [(i, i ^ flip) for i in range(size)])


def across(x, flip):
    sections, size = lax.axis_size("section"), lax.axis_size("seq")
    pairs = [
        (s * size + i, (s ^ 1) * size + (i ^ flip)) for s in range(sections) for i in range(size)
    ]
    return lax.ppermute(x, ("section", "seq"), pairs)


def piece(place, k):
    return (place % 4) ^ (2 * (k // 2) + k % 2)


def after(x, *others):
    return lax.optimization_barrier((x,) + others)[0]


def call(kernel, outs, *args):
    return pl.pallas_call(
        kernel,
        out_shape=outs,
        in_specs=[pl.BlockSpec(memory_space=pltpu.SMEM)]
        + [pl.BlockSpec(memory_space=pltpu.VMEM)] * (len(args) - 1),
        compiler_params=pltpu.CompilerParams(vmem_limit_bytes=VMEM_LIMIT),
        cost_estimate=pl.CostEstimate(flops=1, transcendentals=0, bytes_accessed=1),
    )(*args)


def scale_kernel(place_ref, rows_ref, out_ref):
    rows = rows_ref[...].astype(jnp.float32)
    scale = lax.rsqrt(jnp.mean(rows * rows, axis=1, keepdims=True) + 1e-05)
    out_ref[...] = jnp.broadcast_to(scale, out_ref.shape)


def dot(a, b):
    return jnp.dot(a, b, preferred_element_type=jnp.float32)


def project(place, own_ref, far_ref, gain_ref, weights, pieces):
    half = place // 4
    near = None
    far = None
    for k, weight in zip(pieces, weights):
        width = weight.shape[0]
        part = piece(place, k)
        start = pl.multiple_of(part * width, width)
        whole = pl.multiple_of((half * 4 + part) * width, width)
        gain = gain_ref[:, pl.ds(whole, width)]
        a = (own_ref[:, pl.ds(whole, width)].astype(jnp.float32) * gain).astype(jnp.bfloat16)
        b = (far_ref[:, pl.ds(start, width)].astype(jnp.float32) * gain).astype(jnp.bfloat16)
        w = weight[...]
        total = dot(jnp.concatenate([a, b], axis=0), w)
        a, b = total[: a.shape[0]], total[a.shape[0] :]
        near = a if near is None else near + a
        far = b if far is None else far + b
    return near, far


def project_kernel(place_ref, own_ref, far_ref, gain_ref, w0, w1, w2, w3, near_out, far_out):
    near, far = project(
        place_ref[0], own_ref, far_ref, gain_ref, (w0, w1, w2, w3), (0, 1, 2, 3)
    )
    near_out[...] = near.astype(near_out.dtype)
    far_out[...] = far.astype(jnp.bfloat16)


def rope(values, cosine, sine):
    return values * cosine + pltpu.roll(values, values.shape[1] // 2, axis=1) * sine


def collect_kernel(place_ref, near_ref, far_ref, scale_ref, cos_ref, sin_ref, out_ref):
    total = near_ref[...] + far_ref[...].astype(jnp.float32)
    scale = scale_ref[...]
    size = total.shape[1] // 2
    keys = rope(total[:, :size] * scale, cos_ref[...], sin_ref[...]).astype(jnp.bfloat16)
    values = (total[:, size:] * scale).astype(jnp.bfloat16)
    for k in range(out_ref.shape[0]):
        out_ref[k, :, :size] = keys
        out_ref[k, :, size:] = values


def attend_kernel(
    place_ref, near_ref, far_ref, scale_ref, cos_ref, sin_ref, kv_ref, out_ref
):
    rows, width = near_ref.shape
    length = kv_ref.shape[0]
    size = kv_ref.shape[1] // 2
    keys = kv_ref[:, :size]
    values = kv_ref[:, size:]
    row_ids = place_ref[0] * rows
    row_ids = row_ids + lax.broadcasted_iota(jnp.int32, (rows, length), 0)
    keep = lax.broadcasted_iota(jnp.int32, (rows, length), 1) <= row_ids
    scale = scale_ref[...]
    cosine = cos_ref[...]
    sine = sin_ref[...]
    for head in range(width // size):
        cols = slice(head * size, (head + 1) * size)
        total = (near_ref[:, cols].astype(jnp.float32) + far_ref[:, cols].astype(jnp.float32)) * scale
        query = rope(total, cosine, sine).astype(jnp.bfloat16)
        scores = lax.dot_general(
            query, keys, (((1,), (1,)), ((), ())), preferred_element_type=jnp.float32
        ) * (1.0 / math.sqrt(size))
        scores = jnp.where(keep, scores, jnp.float32(-1e30))
        raised = jnp.exp(scores - jnp.max(scores, axis=1, keepdims=True))
        total = jnp.sum(raised, axis=1, keepdims=True)
        out_ref[:, cols] = (dot(raised.astype(jnp.bfloat16), values) / total).astype(jnp.bfloat16)


def output_kernel(far, place_ref, heads, rows_ref, *refs):
    weights, outs = refs[:4], refs[4:]
    place = place_ref[0]
    base = 0 if far else place // 4 * 4
    for k, weight in enumerate(weights):
        width = weight.shape[1]
        part = piece(place, k)
        start = pl.multiple_of(part * width, width)
        whole = pl.multiple_of((base + part) * width, width)
        total = dot(heads[...], weight[...])
        total = total + rows_ref[:, pl.ds(whole, width)].astype(jnp.float32)
        row = 0
        for out in outs:
            some = total[row : row + out.shape[0]]
            out[:, pl.ds(start, width)] = some.astype(jnp.bfloat16)
            row += out.shape[0]


def assemble_kernel(place_ref, first, second, far, out_ref):
    half = place_ref[0] // 4
    rows, width = first.shape
    near_cols = pl.ds(pl.multiple_of(half * width, width), width)
    out_ref[:rows, near_cols] = first[...]
    out_ref[rows:, near_cols] = second[...]
    out_ref[:, pl.ds(pl.multiple_of((1 - half) * width, width), width)] = far[...]


def at_row(kernel, *fixed):
    def run(*refs):
        kernel(*fixed, *refs)

    return run


def shards(section_input, norm_gain, w_query, w_keyval, w_out, down_grads, up_grads):
    rows = section_input[0]
    tokens, features = rows.shape
    size = w_keyval.shape[2] // 2
    wide = w_query.shape[2]
    bf16, f32 = jnp.bfloat16, jnp.float32
    seq = lax.axis_index("seq")
    half = seq // 4
    place = seq.astype(jnp.int32)[None]

    def array(count, columns, kind=bf16):
        return jax.ShapeDtypeStruct((count, columns), kind)

    sent = lax.dynamic_slice_in_dim(rows, (1 - half) * (features // 2), features // 2, axis=1)
    far_rows = exchange(sent, 4)
    keyval_2 = exchange(w_keyval[0], 2)
    keyval_1 = exchange(w_keyval[0], 1)
    scale = call(scale_kernel, array(tokens, size, f32), place, after(rows, sent))
    w_query = after(w_query[0], scale)
    query_2 = exchange(w_query, 2)
    query_1 = exchange(w_query, 1)
    keyval_3 = exchange(keyval_2, 1)
    query_3 = exchange(query_2, 1)
    out_1 = exchange(after(w_out[0], scale), 1)

    frequency = 10000.0 ** (-(jnp.arange(size // 2, dtype=f32) * 2.0 / size))
    positions = (seq * tokens + jnp.arange(tokens)).astype(f32)
    angles = positions[:, None] * frequency[None, :]
    cosine = jnp.cos(angles)
    sine = jnp.sin(angles)
    cosine = jnp.concatenate([cosine, cosine], axis=1)
    sine = jnp.concatenate([-sine, sine], axis=1)

    near, far = call(
        project_kernel,
        (array(tokens, 2 * size, f32), array(tokens, 2 * size)),
        place, rows, far_rows, norm_gain, w_keyval[0], keyval_1, keyval_2, keyval_3,
    )
    far = exchange(far, 4)
    query_near, query_far = call(
        project_kernel,
        (array(tokens, wide), array(tokens, wide)),
        place, rows, far_rows, norm_gain, w_query, query_1, query_2, query_3,
    )
    keyval = call(
        collect_kernel,
        jax.ShapeDtypeStruct((lax.axis_size("seq"), tokens, 2 * size), bf16),
        place, near, far, scale, cosine, sine,
    )
    keyval = lax.all_to_all(keyval, "seq", split_axis=0, concat_axis=0, tiled=True)
    keyval = keyval.reshape(-1, 2 * size)
    query_far = exchange(query_far, 4)
    heads = call(
        attend_kernel,
        array(tokens, wide),
        place, query_near, query_far, scale, cosine, sine, keyval,
    )
    far_heads = exchange(heads, 4)
    out_2 = exchange(after(w_out[0], query_2), 2)
    out_3 = exchange(after(out_2, heads), 1)
    weights = w_out[0], out_1, out_2, out_3
    half_rows = array(tokens, features // 2)
    parts = tuple(array(n, features // 2) for n in (LEADING, tokens - LEADING))
    near = call(at_row(output_kernel, False), parts, place, heads, rows, *weights)
    far_heads = after(far_heads, *near)
    far = call(at_row(output_kernel, True), half_rows, place, far_heads, far_rows, *weights)
    first = across(near[0], 0)
    received = [first, across(after(near[1], first), 0), across(far, 4)]
    out = call(assemble_kernel, array(tokens, features), place, *received)
    sections = lax.axis_size("section")
    mirrored = lax.ppermute(
        after(up_grads[0], far),
        "section",
        [(i, sections - 1 - i) for i in range(sections)],
    )
    grad_total = (down_grads[0].astype(f32) + mirrored.astype(f32)).astype(bf16)
    return (out[None], grad_total[None])


def solution(mesh):
    return jax.shard_map(
        shards,
        mesh=mesh,
        in_specs=(
            P("section", "seq", None),
            P("section", None),
            P("section", "seq", None),
            P("section", "seq", None),
            P("section", None, "seq"),
            P("section", "seq", None),
            P("section", "seq", None),
        ),
        out_specs=(P("section", "seq", None), P("section", "seq", None)),
        check_vma=False,
    )
```
